32 devices in a mesh: row: 8 (over z, y), col: 4 (over x, core).
Axes of the slice: x: 2, y: 2, z: 4, core: 2. Of those that a mesh axis runs over, the one named last changes fastest.
Arguments:
- queries: bfloat16 [1024, 1024], P('row', 'col'), may hold values from -26 to 26
- key_vectors: bfloat16 [1024, 1024], P('row', 'col'), may hold values from -8 to 8
- values: bfloat16 [1024, 1024], P('row', 'col'), may hold values from -6 to 6
- sink_logit: float32 [8], P('col'), may hold values from -1 to 5
- lengths: int32 [8], replicated, may hold values from 1 to 576, as said below
- stream: bfloat16 [1024, 2048], P('row', 'col'), may hold values from -60 to 60
- out_weight: bfloat16 [1024, 2048], P('col', 'row'), may hold values from -0.1875 to 0.1875
- norm_gain: bfloat16 [2048], P('col'), may hold values from 0.25 to 1.75
- shared_gate: bfloat16 [2048, 2816], P('row', 'col'), may hold values from -0.125 to 0.125
- shared_up: bfloat16 [2048, 2816], P('row', 'col'), may hold values from -0.125 to 0.125
- shared_down: bfloat16 [2816, 2048], P('col', 'row'), may hold values from -0.109375 to 0.109375
- shared_switch: bfloat16 [2048], replicated, may hold values from -0.125 to 0.125
- expert_gate: bfloat16 [8, 2048, 1408], P('row', None, 'col'), may hold values from -0.125 to 0.125
- expert_up: bfloat16 [8, 2048, 1408], P('row', None, 'col'), may hold values from -0.125 to 0.125
- expert_down: bfloat16 [8, 1408, 2048], P('row', 'col'), may hold values from -0.15625 to 0.15625
- routes: int32 [1024, 4], P('row'), may hold values from 0 to 7, all different within a row; in each aligned block of 128 rows (0 to 127, 128 to 255, ...) at most 96 rows name the same one
- route_weights: float32 [1024, 4], P('row'), may hold values from 0.05 to 0.6
Outputs:
- attended: bfloat16 [1024, 1024], P('row', 'col')
- layer_out: bfloat16 [1024, 2048], P('row', 'col')
The draws below stay inside these ranges and needn't reach their ends.
Inputs may be any that keep to these rules, and one draw needn't show every extreme that they name: `routes`: each row names 4 different experts; among the 128 rows of one device (aligned blocks) no expert is named more than 96 times, a bound that some block reaches. The lengths sum to 1024; exactly one prompt has 576 tokens.
All inputs are finite; a program needn't handle non-finite values.
Results may differ from the reference program's by a relative error of at most 0.01.
Values may be sent and summed in bfloat16 or wider, within the bound.
A program may use at most 128 MiB of HBM per device.

```python
import math
import jax
import jax.numpy as jnp
import numpy as np
from jax import lax

D = 2048
FFE = 1408
HEADS = 8
HDIM = 128
SHARED = 2816
TOP = 4
WINDOW = 4096
TOK_DEV = 128
TOKENS = 1024
EXPERTS = 8
LONGEST = 576
DOCS = 8
CAP = 96
N_ROW = 8
N_COL = 4


def draw_lengths(key, part):
    cut_key = jax.random.fold_in(key, 41)
    place_key = jax.random.fold_in(key, 42)
    remaining = TOKENS - LONGEST
    shuffled = jax.random.permutation(cut_key, remaining - 1) + 1
    cuts = jnp.sort(shuffled[:DOCS - 2]).astype(jnp.int32)
    bounds = jnp.concatenate([jnp.zeros((1,), jnp.int32), cuts, jnp.full((1,), remaining, jnp.int32)])
    pieces = (bounds[1:] - bounds[:-1]).astype(jnp.int32)
    where_long = jax.random.randint(place_key, (), 0, DOCS)
    slots = jnp.arange(DOCS, dtype=jnp.int32)
    earlier = pieces[jnp.minimum(slots, DOCS - 2)]
    later = pieces[jnp.maximum(slots - 1, 0)]
    result = jnp.where(slots < where_long, earlier, jnp.where(slots == where_long, LONGEST, later))
    return result.astype(jnp.int32)


def key_table(key):
    inner_key = jax.random.fold_in(key, 21)
    raw_keys = jnp.clip(2.0 * jax.random.normal(inner_key, (TOKENS, HEADS * HDIM)), -8.0, 8.0)
    return raw_keys


def draw_key_vectors(key, part):
    return key_table(key).astype(jnp.bfloat16)


def draw_queries(key, part):
    inner_key = jax.random.fold_in(key, 22)
    raw_queries = jnp.clip(jax.random.normal(inner_key, (TOKENS, HEADS * HDIM)), -4.0, 4.0)
    return raw_queries.astype(jnp.bfloat16)


def draw_stream(key, part):
    noise_key = jax.random.fold_in(key, 31)
    line_key = jax.random.fold_in(key, 32)
    column_key = jax.random.fold_in(key, 33)
    line_scale = jnp.exp(jax.random.uniform(line_key, (TOKENS, 1), minval=math.log(0.3), maxval=math.log(3.0)))
    column_rough = jnp.exp(jax.random.uniform(column_key, (1, D), minval=math.log(0.5), maxval=math.log(2.0)))
    column_place = (jnp.arange(D, dtype=jnp.float32) / D)[None, :]
    column_scale = column_rough * 0.4 * jnp.exp(math.log(6.0) * column_place)
    noise = jnp.clip(jax.random.normal(noise_key, (TOKENS, D)), -4.0, 4.0)
    result = noise * line_scale * column_scale
    return result.astype(jnp.bfloat16)


def shard_levels(rng, dims, cuts, low, top_value):
    def one(position, shards_of):
        draws = jax.random.uniform(jax.random.fold_in(jax.random.fold_in(rng, 6), position), (shards_of,), jnp.float32, low / len(cuts), top_value / len(cuts))
        return jnp.repeat(jnp.exp(draws), dims[position] // shards_of).reshape((-1,) + (1,) * (len(dims) - position - 1))

    level = one(*cuts[0])
    for cut in cuts[1:]:
        level = level * one(*cut)
    return level


def routed_block(stream_key, own, number, rows, count, top, limit, slope):
    ranking = jax.random.permutation(stream_key, count)
    crowded, usual = load_shares(count, rows * top, limit, slope, True), load_shares(count, rows * top, limit, slope, False)
    places = jnp.arange(count)

    def named(sizes, turn):
        used = int((sizes > 0).sum())
        fixed = max(1, used // 4)
        moved = fixed + (places - fixed + turn * (used - fixed)) % max(1, count - fixed)
        return jnp.zeros((count,), jnp.int32).at[ranking[jnp.where(places < fixed, places, moved)]].set(jnp.asarray(sizes, jnp.int32))

    sizes = jnp.where(number % 4 == 0, named(crowded, number // 4), named(usual, number - number // 4 - 1))
    mixed = jax.random.permutation(jax.random.fold_in(own, 3), count)
    donor, receiver = mixed[0:count // 2 * 2:2], mixed[1:count // 2 * 2:2]
    slack = jnp.minimum(sizes[donor] - 1, limit - sizes[receiver]) // 2
    slack = jnp.where((donor == ranking[0]) | (receiver == ranking[0]) | (sizes[receiver] == 0), 0, jnp.maximum(slack, 0))
    moved = jax.random.randint(jax.random.fold_in(own, 4), (count // 2,), 0, 1 << 20) % (slack + 1)
    sizes = sizes.at[donor].add(-moved).at[receiver].add(moved)
    members = jnp.searchsorted(jnp.cumsum(sizes), jnp.arange(rows * top), side="right").astype(jnp.int32)
    grid = members.reshape(top, rows).T
    grid = grid[jax.random.permutation(jax.random.fold_in(own, 1), rows)]
    turn = jax.random.randint(jax.random.fold_in(own, 2), (rows, 1), 0, top)
    return jnp.take_along_axis(grid, (jnp.arange(top)[None, :] + turn) % top, axis=1)


def load_shares(number_of, total, bound, skew, full):
    portions = [(1 << 20) // math.isqrt(standing ** skew) + 1 for standing in range(1, number_of + 1)]
    largest = bound if full else min(bound, max(-(-total // number_of), total * portions[0] // sum(portions)))
    least = 1 if total - largest >= number_of - 1 else 0
    given, spare = [largest] + [least] * (number_of - 1), total - largest - least * (number_of - 1)
    while spare > 0:
        free = [i for i in range(1, number_of) if given[i] < largest] or [i for i in range(1, number_of) if given[i] < bound]
        pool, left = sum([portions[i] for i in free]), spare
        for i in free:
            addition = min(bound - given[i], max(1, left * portions[i] // pool), spare)
            given[i] = given[i] + addition
            spare = spare - addition
    return np.array(given)


def normal_values(stream_key, shape, scale, reach, split=(), held_as=jnp.bfloat16):
    level = shard_levels(stream_key, shape, split, -0.22, 0.18) if split else 1.0
    drawn = jax.random.normal(stream_key, shape, jnp.float32) * scale * level
    return jnp.minimum(jnp.maximum(drawn, -reach), reach).astype(held_as)


def setup_inputs(seed: int = 0) -> dict:
    seeds = jax.random.split(jax.random.key(seed), 18)
    queries = draw_queries(jax.random.fold_in(seeds[17], 71), 0)
    key_vectors = draw_key_vectors(jax.random.fold_in(seeds[17], 71), 0)
    values = normal_values(seeds[2], (TOKENS, HEADS * HDIM), 1.0, 6.0, ((0, 8), (1, 4)))
    sink_logit = jnp.clip(-1.0 + 6.0 * jax.random.uniform(seeds[3], (HEADS,), jnp.float32) ** shard_levels(seeds[3], (HEADS,), ((0, 4),), -0.2, 0.2), -1.0, 5.0)
    lengths = draw_lengths(jax.random.fold_in(seeds[17], 71), 0)
    stream = draw_stream(jax.random.fold_in(seeds[17], 71), 0)
    out_weight = normal_values(seeds[6], (HEADS * HDIM, D), (HEADS * HDIM) ** -0.5, 0.1875, ((0, 4), (1, 8)))
    norm_gain = jnp.clip(1.0 + 0.15 * jax.random.normal(seeds[7], (D,), jnp.float32), 0.25, 1.75).astype(jnp.bfloat16)
    shared_gate = normal_values(seeds[8], (D, SHARED), D ** -0.5, 0.125, ((0, 8), (1, 4)))
    shared_up = normal_values(seeds[9], (D, SHARED), D ** -0.5, 0.125, ((0, 8), (1, 4)))
    shared_down = normal_values(seeds[10], (SHARED, D), SHARED ** -0.5, 0.109375, ((0, 4), (1, 8)))
    shared_switch = normal_values(seeds[11], (D,), D ** -0.5, 0.125)
    expert_gate = normal_values(seeds[12], (EXPERTS, D, FFE), D ** -0.5, 0.125, ((0, 8), (2, 4)))
    expert_up = normal_values(seeds[13], (EXPERTS, D, FFE), D ** -0.5, 0.125, ((0, 8), (2, 4)))
    expert_down = normal_values(seeds[14], (EXPERTS, FFE, D), FFE ** -0.5, 0.15625, ((0, 8), (1, 4)))
    routes_keys = jax.random.split(jax.random.fold_in(seeds[15], 1), TOKENS // TOK_DEV)
    routes_turns = jax.random.permutation(jax.random.fold_in(seeds[15], 3), TOKENS // TOK_DEV)
    routes = jax.vmap(lambda own, number: routed_block(jax.random.fold_in(seeds[15], 2), own, number, TOK_DEV, EXPERTS, TOP, CAP, 2))(routes_keys, routes_turns).reshape((TOKENS, TOP))
    route_weights = jnp.clip(jnp.exp(math.log(0.6) - 2.4849067 * jax.random.uniform(seeds[16], (TOKENS, TOP), jnp.float32) ** shard_levels(seeds[16], (TOKENS, TOP), ((0, 8),), -0.2, 0.2)), 0.05, 0.6)
    return {"queries": queries, "key_vectors": key_vectors, "values": values, "sink_logit": sink_logit, "lengths": lengths, "stream": stream, "out_weight": out_weight, "norm_gain": norm_gain, "shared_gate": shared_gate, "shared_up": shared_up, "shared_down": shared_down, "shared_switch": shared_switch, "expert_gate": expert_gate, "expert_up": expert_up, "expert_down": expert_down, "routes": routes, "route_weights": route_weights}


norm_eps = 1e-06
masked_score = -1e+30

def lower_bounds(lengths, positions):
    doc_ends = jnp.cumsum(lengths).astype(jnp.int32)
    starts = (doc_ends - lengths).astype(jnp.int32)
    begun_docs = starts[None, :] <= positions[:, None]
    doc_start = lax.optimization_barrier(jnp.max(jnp.where(begun_docs, starts[None, :], 0), axis=1)).astype(jnp.int32)
    return jnp.maximum(doc_start, positions - WINDOW + 1).astype(jnp.int32)

def attend(queries, key_vectors, values, sink_logit, lower_bound):
    span = min(512, TOKENS)
    score_scale = 1.0 / math.sqrt(HDIM)
    key_heads = key_vectors.reshape(TOKENS, HEADS, HDIM).astype(jnp.float32)
    value_heads = values.reshape(TOKENS, HEADS, HDIM).astype(jnp.float32)
    key_places = jnp.arange(TOKENS, dtype=jnp.int32)

    def one_block(block_index):
        first_row = block_index * span
        query_block = lax.dynamic_slice_in_dim(queries, first_row, span, 0).reshape(span, HEADS, HDIM).astype(jnp.float32)
        low_bound = lax.dynamic_slice_in_dim(lower_bound, first_row, span, 0)
        positions = first_row + jnp.arange(span, dtype=jnp.int32)
        scores = jnp.einsum('qhd,khd->hqk', query_block, key_heads) * score_scale
        visible = ((key_places[None, :] >= low_bound[:, None]) & (key_places[None, :] <= positions[:, None]))[None]
        masked = jnp.where(visible, scores, masked_score)
        row_max = jnp.maximum(lax.optimization_barrier(jnp.max(masked, axis=2)), sink_logit[:, None])
        weight = jnp.where(visible, jnp.exp(masked - row_max[:, :, None]), 0.0)
        denominator = lax.optimization_barrier(jnp.sum(weight, axis=2)) + jnp.exp(sink_logit[:, None] - row_max)
        rounded = lax.optimization_barrier(weight.astype(jnp.bfloat16)).astype(jnp.float32)
        mixture = jnp.einsum('hqk,khd->hqd', rounded, value_heads) / denominator[:, :, None]
        return jnp.transpose(mixture, (1, 0, 2)).reshape(span, HEADS * HDIM).astype(jnp.bfloat16)
    blocks = lax.map(one_block, jnp.arange(TOKENS // span, dtype=jnp.int32))
    return blocks.reshape(TOKENS, HEADS * HDIM)

def expert_table(routes):
    flat_routes = routes.reshape(N_ROW, TOK_DEV * TOP)
    onehot = (flat_routes[:, :, None] == jnp.arange(EXPERTS, dtype=jnp.int32)[None, None, :]).astype(jnp.int32)
    before = (jnp.cumsum(onehot, axis=1) - onehot).astype(jnp.int32)
    slot_index = lax.optimization_barrier(jnp.sum(before * onehot, axis=2)).astype(jnp.int32)
    device_block = jnp.arange(N_ROW, dtype=jnp.int32)[:, None]
    target = (flat_routes * (N_ROW * CAP) + device_block * CAP + slot_index).reshape(-1).astype(jnp.int32)
    owner_row = (jnp.arange(TOKENS * TOP, dtype=jnp.int32) // TOP).astype(jnp.int32)
    source = jnp.full((EXPERTS * N_ROW * CAP,), TOKENS, jnp.int32).at[target].set(owner_row)
    return (target, source)

def experts_apply(normed, routes, route_weights, expert_gate, expert_up, expert_down):
    target, source = expert_table(routes)
    slot_weight = jnp.zeros((EXPERTS * N_ROW * CAP,), jnp.float32).at[target].set(route_weights.reshape(-1))
    padded = jnp.concatenate([normed, jnp.zeros((1, D), jnp.bfloat16)], 0)
    source = source.reshape(EXPERTS, N_ROW * CAP)
    slot_weight = slot_weight.reshape(EXPERTS, N_ROW * CAP)
    group = FFE // N_COL

    def per_expert(accum, expert_index):
        picked = source[expert_index]
        dispatched = padded[picked]
        gate_out = jnp.dot(dispatched, expert_gate[expert_index], preferred_element_type=jnp.float32)
        up_out = jnp.dot(dispatched, expert_up[expert_index], preferred_element_type=jnp.float32)
        activation = (jax.nn.silu(gate_out) * up_out).astype(jnp.bfloat16)
        partials = jnp.einsum('mcf,cfd->cmd', activation.reshape(-1, N_COL, group).astype(jnp.float32), expert_down[expert_index].reshape(N_COL, group, D).astype(jnp.float32))
        part_sum = lax.optimization_barrier(jnp.sum(lax.optimization_barrier(partials.astype(jnp.bfloat16)).astype(jnp.float32), axis=0))
        accum = accum.at[picked].add(slot_weight[expert_index][:, None] * part_sum)
        return (accum, None)
    accum, unused = lax.scan(per_expert, jnp.zeros((TOKENS + 1, D), jnp.float32), jnp.arange(EXPERTS, dtype=jnp.int32))
    return accum[:TOKENS]

def reference(queries, key_vectors, values, sink_logit, lengths, stream, out_weight, norm_gain, shared_gate, shared_up, shared_down, shared_switch, expert_gate, expert_up, expert_down, routes, route_weights):
    positions = jnp.arange(TOKENS, dtype=jnp.int32)
    lower_bound = lower_bounds(lengths, positions)
    attended = attend(queries, key_vectors, values, sink_logit, lower_bound)
    hidden = (stream.astype(jnp.float32) + jnp.dot(attended, out_weight, preferred_element_type=jnp.float32)).astype(jnp.bfloat16)
    widened = hidden.astype(jnp.float32)
    normed = (widened * lax.rsqrt(lax.optimization_barrier(jnp.mean(widened * widened, axis=1, keepdims=True)) + norm_eps) * norm_gain.astype(jnp.float32)).astype(jnp.bfloat16)
    shared_gate_out = jnp.dot(normed, shared_gate, preferred_element_type=jnp.float32)
    shared_up_out = jnp.dot(normed, shared_up, preferred_element_type=jnp.float32)
    shared_act = (jax.nn.silu(shared_gate_out) * shared_up_out).astype(jnp.bfloat16)
    shared_out = jnp.dot(shared_act, shared_down, preferred_element_type=jnp.float32)
    switch = jax.nn.sigmoid(jnp.dot(normed, shared_switch, preferred_element_type=jnp.float32))
    routed = experts_apply(normed, routes, route_weights, expert_gate, expert_up, expert_down)
    layer_out = (widened + switch[:, None] * shared_out + routed).astype(jnp.bfloat16)
    return (attended, layer_out)
```

```python
import math

import jax
import jax.numpy as jnp
from jax import lax
from jax.experimental import pallas as pl
from jax.experimental.pallas import tpu as pltpu
from jax.sharding import PartitionSpec as P

HDIM = 128
WINDOW = 4096


norm_eps = 1e-06
masked_score = -1e30


def lower_bounds(lengths, positions):
    doc_ends = jnp.cumsum(lengths)
    starts = doc_ends - lengths
    begun_docs = starts[None, :] <= positions[:, None]
    doc_start = jnp.max(jnp.where(begun_docs, starts[None, :], 0), axis=1)
    return jnp.maximum(doc_start, positions - WINDOW + 1)


MESH = pl.DeviceIdType.MESH
LONGEST = 576
ROWS = 8
COLS = 4
TOK = 128
WIDTH = 2048
PART = WIDTH // COLS
SLICE = WIDTH // ROWS
UNITS = 96
REACH = (LONGEST - 2 + TOK) // TOK
NT = (((1,), (1,)), ((), ()))


def mm(a, b):
    return jnp.dot(a, b, preferred_element_type=jnp.float32)


def layer_kernel(
    q_ref,
    k_ref,
    v_ref,
    sink_ref,
    lower_ref,
    stream_ref,
    wo_ref,
    gain_ref,
    sh_ref,
    switch_ref,
    eg_ref,
    eu_ref,
    ed_ref,
    w_ref,
    att_ref,
    out_ref,
    kv_buf,
    wo_buf,
    gain_buf,
    sh_buf,
    w_buf,
    head_send,
    head_recv,
    hid,
    own_hidden,
    keep_a,
    keep_b,
    send1,
    recv1,
    send2,
    recv2,
    send3,
    recv3,
    s_kv,
    r_kv,
    s_wo,
    r_wo,
    s_gain,
    r_gain,
    s_sh,
    r_sh,
    s_w,
    r_w,
    s_head,
    r_head,
    s_row,
    r_row,
    s_core,
    r_core,
    s_x,
    r_x,
    s_fwd,
    r_fwd,
    s_1,
    r_1,
    s_2,
    r_2,
    s_3,
    r_3,
):
    r = lax.axis_index("row")
    c = lax.axis_index("col")
    core_peer = c + 1 - 2 * (c % 2)
    x_peer = (c + 2) % COLS
    far_peer = (core_peer + 2) % COLS

    def up(k):
        return (r + k) % ROWS

    def down(k):
        return (r + ROWS - k) % ROWS

    def cols(i, n):
        return pl.ds(pl.multiple_of(i * n, n), n)

    barrier = pltpu.get_barrier_semaphore()
    for k in range(1, ROWS):
        pl.semaphore_signal(barrier, inc=1, device_id=(up(k), c), device_id_type=MESH)
    for k in range(1, COLS):
        pl.semaphore_signal(barrier, inc=1, device_id=(r, (c + k) % COLS), device_id_type=MESH)
    pl.semaphore_wait(barrier, ROWS - 1 + COLS - 1)

    def push(src, dst, send, recv, where):
        return pltpu.make_async_remote_copy(
            src_ref=src,
            dst_ref=dst,
            send_sem=send,
            recv_sem=recv,
            device_id=where,
            device_id_type=MESH,
        )

    def k_copy(k):
        return push(
            k_ref, kv_buf.at[0, pl.ds(k * TOK, TOK)], s_kv.at[0, k], r_kv.at[0, k], (up(k), c)
        )

    def v_copy(k):
        return push(
            v_ref, kv_buf.at[1, pl.ds(k * TOK, TOK)], s_kv.at[1, k], r_kv.at[1, k], (up(k), c)
        )

    def wo_copy(k, block):
        return push(wo_ref, wo_buf.at[:, cols(block, SLICE)], s_wo.at[k], r_wo.at[k], (up(k), c))

    def sh_copy(k, block):
        return push(
            sh_ref.at[up(k)],
            sh_buf.at[:, :, cols(block, SLICE)],
            s_sh.at[k],
            r_sh.at[k],
            (up(k), c),
        )

    def w_copy(k):
        return push(w_ref.at[up(k)], w_buf.at[k], s_w.at[k], r_w.at[k], (up(k), c))

    def gain_copy(k, block):
        return push(
            gain_ref,
            gain_buf.at[:, cols(block, PART)],
            s_gain.at[k],
            r_gain.at[k],
            (r, (c + k) % COLS),
        )

    def head_copy(k):
        return push(
            head_send.at[k], head_recv.at[k], s_head.at[k], r_head.at[k], (r, (c + k) % COLS)
        )

    for k in range(1, REACH + 1):

        @pl.when(r + k < ROWS)
        def _():
            k_copy(k).start()
            v_copy(k).start()

    for k in range(1, ROWS):
        wo_copy(k, r).start()
    for k in range(1, COLS):
        gain_copy(k, c).start()
    for k in range(1, ROWS):
        w_copy(k).start()
    for k in range(1, ROWS):
        sh_copy(k, r).start()

    kv_buf[0, 0:TOK] = k_ref[...]
    kv_buf[1, 0:TOK] = v_ref[...]
    wo_buf[:, cols(r, SLICE)] = wo_ref[...]
    gain_buf[:, cols(c, PART)] = gain_ref[...]
    sh_buf[:, :, cols(r, SLICE)] = sh_ref[r]
    w_buf[0] = w_ref[r]

    for k in range(1, REACH + 1):

        @pl.when(r >= k)
        def _():
            k_copy(k).wait_recv()
            v_copy(k).wait_recv()

        @pl.when(r < k)
        def _():
            kv_buf[:, k * TOK : (k + 1) * TOK] = jnp.zeros((2, TOK, 2 * HDIM), jnp.bfloat16)

    keys = (REACH + 1) * TOK
    place = lax.broadcasted_iota(jnp.int32, (TOK, keys), 1)
    key_place = (r - place // TOK) * TOK + place % TOK
    positions = r * TOK + lax.broadcasted_iota(jnp.int32, (TOK, keys), 0)
    visible = (key_place >= lower_ref[...]) & (key_place <= positions)
    for h in range(2):
        lanes = slice(h * HDIM, (h + 1) * HDIM)
        scores = lax.dot_general(
            q_ref[:, lanes], kv_buf[0, :, lanes], NT, preferred_element_type=jnp.float32
        ) * (1.0 / math.sqrt(HDIM))
        masked = jnp.where(visible, scores, masked_score)
        sink = sink_ref[0:1, h * HDIM : h * HDIM + 1]
        row_max = jnp.maximum(jnp.max(masked, axis=1, keepdims=True), sink)
        weight = jnp.where(visible, jnp.exp(masked - row_max), 0.0)
        denominator = jnp.exp(sink - row_max) + jnp.sum(weight, axis=1, keepdims=True)
        mixture = mm(weight.astype(jnp.bfloat16), kv_buf[1, :, lanes])
        att_ref[:, lanes] = (mixture / denominator).astype(jnp.bfloat16)

    for k in range(1, ROWS):
        wo_copy(k, down(k)).wait_recv()
    attended = att_ref[...]
    for k in range(1, COLS):
        head_send[k] = mm(attended, wo_buf[:, cols((c + k) % COLS, PART)]).astype(jnp.bfloat16)
        head_copy(k).start()
    total = stream_ref[...].astype(jnp.float32) + mm(attended, wo_buf[:, cols(c, PART)])
    for k in range(1, COLS):
        head_copy(k).wait_recv()
        total = total + head_recv[k].astype(jnp.float32)
    hidden = total.astype(jnp.bfloat16)
    own_hidden[...] = hidden
    hid[cols(r, TOK), cols(c, PART)] = hidden

    def row_copy(k, block):
        return push(
            own_hidden,
            hid.at[cols(block, TOK), cols(c, PART)],
            s_row.at[k],
            r_row.at[k],
            (up(k), c),
        )

    def side_copy(k, col, send, recv, peer):
        piece = hid.at[cols(down(k), TOK), cols(col, PART)]
        return push(piece, piece, send.at[k], recv.at[k], (r, peer))

    def copy1(k):
        return push(send1.at[k], recv1.at[k], s_1.at[k], r_1.at[k], (r, core_peer))

    def copy2(k):
        return push(send2.at[k], recv2.at[k], s_2.at[k], r_2.at[k], (r, x_peer))

    def copy3(k):
        return push(send3.at[k], recv3.at[k], s_3.at[k], r_3.at[k], (down(k), c))

    for k in range(1, ROWS):
        row_copy(k, r).start()

    for k in range(1, ROWS):
        sh_copy(k, down(k)).wait_recv()
        w_copy(k).wait_recv()
    for k in range(1, COLS):
        gain_copy(k, (c + COLS - k) % COLS).wait_recv()

    def experts(k):
        widened = hid[cols(down(k), TOK), :].astype(jnp.float32)
        mean = jnp.mean(widened * widened, axis=1, keepdims=True)
        normed = (widened * lax.rsqrt(mean + norm_eps) * gain_buf[0:1, :]).astype(jnp.bfloat16)
        logit = jnp.sum(
            normed.astype(jnp.float32) * switch_ref[...].astype(jnp.float32), axis=1, keepdims=True
        )
        switch = 1.0 / (1.0 + jnp.exp(-logit))
        weights = jnp.broadcast_to(w_buf[k, 0:1, :], (TOK, TOK)).T[:, 0:1]
        gate = mm(normed, eg_ref[...])
        act = gate / (1.0 + jnp.exp(-gate)) * mm(normed, eu_ref[...])
        act = (act * weights).astype(jnp.bfloat16)
        gate = lax.dot_general(normed, sh_buf[0], NT, preferred_element_type=jnp.float32)
        raised = lax.dot_general(normed, sh_buf[1], NT, preferred_element_type=jnp.float32)
        shared = (gate / (1.0 + jnp.exp(-gate)) * raised * switch).astype(jnp.bfloat16)

        def term(col):
            lanes = cols(col, PART)
            return mm(act, ed_ref[:, lanes]) + mm(shared, sh_buf[2, :, lanes])

        send1[k, 0] = term(core_peer).astype(jnp.bfloat16)
        send1[k, 1] = term(far_peer).astype(jnp.bfloat16)
        copy1(k).start()
        keep_b[k] = term(x_peer)
        keep_a[k] = term(c)

    def step(s, carry):
        @pl.when(s < ROWS)
        def _():
            @pl.when(s > 0)
            def _():
                row_copy(s, down(s)).wait_recv()

            side_copy(s, c, s_core, r_core, core_peer).start()
            side_copy(s, c, s_x, r_x, x_peer).start()

        @pl.when((s >= 1) & (s < ROWS + 1))
        def _():
            side_copy(s - 1, x_peer, s_x, r_x, x_peer).wait_recv()
            side_copy(s - 1, x_peer, s_fwd, r_fwd, core_peer).start()

        @pl.when((s >= 2) & (s < ROWS + 2))
        def _():
            side_copy(s - 2, core_peer, s_core, r_core, core_peer).wait_recv()
            side_copy(s - 2, far_peer, s_fwd, r_fwd, core_peer).wait_recv()
            experts(s - 2)

        @pl.when((s >= 3) & (s < ROWS + 3))
        def _():
            k = s - 3
            copy1(k).wait_recv()
            send2[k] = (keep_b[k] + recv1[k, 1].astype(jnp.float32)).astype(jnp.bfloat16)
            copy2(k).start()
            keep_a[k] = keep_a[k] + recv1[k, 0].astype(jnp.float32)

        @pl.when(s >= 4)
        def _():
            k = s - 4
            copy2(k).wait_recv()
            done = keep_a[k] + recv2[k].astype(jnp.float32)
            keep_a[k] = done

            @pl.when(k > 0)
            def _():
                send3[k] = done.astype(jnp.bfloat16)
                copy3(k).start()

        return carry

    lax.fori_loop(0, ROWS + 4, step, 0)

    total = own_hidden[...].astype(jnp.float32) + keep_a[0]
    for k in range(1, ROWS):
        copy3(k).wait_recv()
        total = total + recv3[k].astype(jnp.float32)
    out_ref[...] = total.astype(jnp.bfloat16)

    for k in range(1, REACH + 1):

        @pl.when(r + k < ROWS)
        def _():
            k_copy(k).wait_send()
            v_copy(k).wait_send()

    for k in range(1, COLS):
        gain_copy(k, c).wait_send()
        head_copy(k).wait_send()
    for k in range(ROWS):
        if k > 0:
            wo_copy(k, r).wait_send()
            w_copy(k).wait_send()
            sh_copy(k, r).wait_send()
            row_copy(k, r).wait_send()
            copy3(k).wait_send()
        side_copy(k, c, s_core, r_core, core_peer).wait_send()
        side_copy(k, c, s_x, r_x, x_peer).wait_send()
        side_copy(k, x_peer, s_fwd, r_fwd, core_peer).wait_send()
        copy1(k).wait_send()
        copy2(k).wait_send()


def fused_body(
    queries,
    key_vectors,
    values,
    sink_logit,
    lengths,
    stream,
    out_weight,
    norm_gain,
    shared_gate,
    shared_up,
    shared_down,
    shared_switch,
    expert_gate,
    expert_up,
    expert_down,
    routes,
    route_weights,
):
    my_row = lax.axis_index("row")
    positions = my_row * TOK + jnp.arange(TOK, dtype=jnp.int32)
    lower = lower_bounds(lengths, positions)[:, None]
    sink = jnp.broadcast_to(jnp.repeat(sink_logit, HDIM)[None, :], (8, 2 * HDIM))
    gain = jnp.broadcast_to(norm_gain.astype(jnp.float32)[None, :], (8, PART))
    units = shared_gate.shape[1] // ROWS
    shared = jnp.stack(
        [
            shared_gate.T.reshape(ROWS, units, SLICE),
            shared_up.T.reshape(ROWS, units, SLICE),
            shared_down.reshape(ROWS, units, SLICE),
        ],
        1,
    )
    shared = jnp.pad(shared, ((0, 0), (0, 0), (0, UNITS - units), (0, 0)))
    expert_ids = jnp.arange(ROWS, dtype=jnp.int32)
    token_weights = jnp.sum(
        jnp.where(routes[None, :, :] == expert_ids[:, None, None], route_weights[None], 0.0), axis=2
    )
    token_weights = jnp.broadcast_to(token_weights[:, None, :], (ROWS, 8, TOK))
    bf16, f32 = jnp.bfloat16, jnp.float32
    eight = pltpu.SemaphoreType.DMA((ROWS,))
    four = pltpu.SemaphoreType.DMA((COLS,))
    pair = pltpu.SemaphoreType.DMA((2, ROWS))
    vmem = pl.BlockSpec(memory_space=pltpu.VMEM)
    return pl.pallas_call(
        layer_kernel,
        out_shape=(
            jax.ShapeDtypeStruct(queries.shape, bf16),
            jax.ShapeDtypeStruct(stream.shape, bf16),
        ),
        in_specs=[vmem] * 14,
        out_specs=(vmem, vmem),
        scratch_shapes=[
            pltpu.VMEM((2, (REACH + 1) * TOK, 2 * HDIM), bf16),
            pltpu.VMEM((2 * HDIM, WIDTH), bf16),
            pltpu.VMEM((8, WIDTH), f32),
            pltpu.VMEM((3, UNITS, WIDTH), bf16),
            pltpu.VMEM((ROWS, 8, TOK), f32),
            pltpu.VMEM((COLS, TOK, PART), bf16),
            pltpu.VMEM((COLS, TOK, PART), bf16),
            pltpu.VMEM((ROWS * TOK, WIDTH), bf16),
            pltpu.VMEM((TOK, PART), bf16),
            pltpu.VMEM((ROWS, TOK, PART), f32),
            pltpu.VMEM((ROWS, TOK, PART), f32),
            pltpu.VMEM((ROWS, 2, TOK, PART), bf16),
            pltpu.VMEM((ROWS, 2, TOK, PART), bf16),
            pltpu.VMEM((ROWS, TOK, PART), bf16),
            pltpu.VMEM((ROWS, TOK, PART), bf16),
            pltpu.VMEM((ROWS, TOK, PART), bf16),
            pltpu.VMEM((ROWS, TOK, PART), bf16),
            pair,
            pair,
            eight,
            eight,
            four,
            four,
            eight,
            eight,
            eight,
            eight,
            four,
            four,
        ]
        + [eight] * 14,
        compiler_params=pltpu.CompilerParams(
            collective_id=0, has_side_effects=True, vmem_limit_bytes=50 << 20
        ),
    )(
        queries,
        key_vectors,
        values,
        sink,
        lower,
        stream,
        out_weight,
        gain,
        shared,
        shared_switch[None, :],
        expert_gate[0],
        expert_up[0],
        expert_down[0],
        token_weights,
    )


def gathered_body(
    queries,
    key_vectors,
    values,
    sink_logit,
    lengths,
    stream,
    out_weight,
    norm_gain,
    shared_gate,
    shared_up,
    shared_down,
    shared_switch,
    expert_gate,
    expert_up,
    expert_down,
    routes,
    route_weights,
):
    local_tokens = queries.shape[0]
    feature_width = queries.shape[1]
    head_count = feature_width // HDIM
    my_row = lax.axis_index("row")
    positions = my_row * local_tokens + jnp.arange(local_tokens, dtype=jnp.int32)
    lower_bound = lower_bounds(lengths, positions)
    query_heads = queries.reshape(local_tokens, head_count, HDIM)
    score_scale = 1.0 / math.sqrt(HDIM)
    key_value = jnp.stack([key_vectors, values], 0)
    key_piece = lax.all_gather(key_value, "row", axis=1, tiled=True)
    row_max = jnp.broadcast_to(sink_logit[None, :], (local_tokens, head_count))
    denominator = jnp.ones((local_tokens, head_count), jnp.float32)
    numerator = jnp.zeros((local_tokens, head_count, HDIM), jnp.float32)
    needed = key_piece.shape[1]
    key_heads = key_piece[0].reshape(needed, head_count, HDIM)
    value_heads = key_piece[1].reshape(needed, head_count, HDIM)
    scores = (
        jnp.einsum("qhd,khd->qhk", query_heads, key_heads, preferred_element_type=jnp.float32)
        * score_scale
    )
    key_places = jnp.arange(needed, dtype=jnp.int32)
    visible = (
        (key_places[None, :] >= lower_bound[:, None]) & (key_places[None, :] <= positions[:, None])
    )[:, None, :]
    masked = jnp.where(visible, scores, masked_score)
    new_max = jnp.maximum(row_max, jnp.max(masked, axis=2))
    weight = jnp.where(visible, jnp.exp(masked - new_max[:, :, None]), 0.0)
    rescale = jnp.exp(row_max - new_max)
    denominator = denominator * rescale + jnp.sum(weight, axis=2)
    numerator = numerator * rescale[:, :, None] + jnp.einsum(
        "qhk,khd->qhd", weight.astype(jnp.bfloat16), value_heads, preferred_element_type=jnp.float32
    )
    final_max, denominator, numerator = (new_max, denominator, numerator)
    attended = (
        (numerator / denominator[:, :, None])
        .reshape(local_tokens, feature_width)
        .astype(jnp.bfloat16)
    )
    head_terms = jnp.dot(
        attended,
        lax.all_gather(out_weight, "row", axis=1, tiled=True),
        preferred_element_type=jnp.float32,
    )
    mixed_heads = lax.psum_scatter(
        head_terms.astype(jnp.bfloat16), "col", scatter_dimension=1, tiled=True
    ).astype(jnp.float32)
    hidden = (stream.astype(jnp.float32) + mixed_heads).astype(jnp.bfloat16)
    widened = hidden.astype(jnp.float32)
    full_width = lax.axis_size("col") * hidden.shape[1]
    squares = lax.psum(jnp.sum(widened * widened, axis=1), "col")
    row_scale = lax.rsqrt(squares / full_width + norm_eps)
    normed_part = (widened * row_scale[:, None] * norm_gain.astype(jnp.float32)).astype(
        jnp.bfloat16
    )
    normed = lax.all_gather(normed_part, "col", axis=1, tiled=True)
    gate_part = jnp.dot(
        normed,
        lax.all_gather(shared_gate, "row", axis=0, tiled=True),
        preferred_element_type=jnp.float32,
    )
    up_part = jnp.dot(
        normed,
        lax.all_gather(shared_up, "row", axis=0, tiled=True),
        preferred_element_type=jnp.float32,
    )
    shared_act = (jax.nn.silu(gate_part) * up_part).astype(jnp.bfloat16)
    shared_part = jnp.dot(
        shared_act,
        lax.all_gather(shared_down, "row", axis=1, tiled=True),
        preferred_element_type=jnp.float32,
    )
    switch = jax.nn.sigmoid(jnp.dot(normed, shared_switch, preferred_element_type=jnp.float32))
    row_count = lax.axis_size("row")
    fanout = routes.shape[1]
    model_width = normed.shape[1]
    capacity = max(2, min(local_tokens, 3 * local_tokens * fanout // (2 * row_count)))
    flat_routes = routes.reshape(-1)
    onehot = (flat_routes[:, None] == jnp.arange(row_count, dtype=jnp.int32)[None, :]).astype(
        jnp.int32
    )
    before = jnp.cumsum(onehot, axis=0) - onehot
    slot_index = jnp.sum(before * onehot, axis=1)
    target = flat_routes * capacity + slot_index
    owner_row = jnp.arange(local_tokens * fanout, dtype=jnp.int32) // fanout
    source = jnp.full((row_count * capacity,), local_tokens, jnp.int32).at[target].set(owner_row)
    padded = jnp.concatenate([normed, jnp.zeros((1, model_width), jnp.bfloat16)], 0)
    outgoing = padded[source].reshape(row_count, capacity, model_width)
    received = lax.all_to_all(outgoing, "row", split_axis=0, concat_axis=0, tiled=True)
    senders, slot_count, received_width = received.shape
    dispatched = received.reshape(senders * slot_count, received_width)
    gate_out = jnp.dot(dispatched, expert_gate[0], preferred_element_type=jnp.float32)
    up_out = jnp.dot(dispatched, expert_up[0], preferred_element_type=jnp.float32)
    activation = (jax.nn.silu(gate_out) * up_out).astype(jnp.bfloat16)
    partial_out = jnp.dot(activation, expert_down[0], preferred_element_type=jnp.float32).astype(
        jnp.bfloat16
    )
    returned = lax.all_to_all(
        partial_out.reshape(senders, slot_count, received_width),
        "row",
        split_axis=0,
        concat_axis=0,
        tiled=True,
    )
    route_rows = returned.reshape(row_count * capacity, model_width)[target].reshape(
        local_tokens, fanout, model_width
    )
    routed = jnp.zeros((local_tokens, model_width), jnp.float32)
    for route_slot in range(fanout):
        routed = routed + route_weights[:, route_slot][:, None] * route_rows[
            :, route_slot, :
        ].astype(jnp.float32)
    layer_terms = switch[:, None] * shared_part + routed
    summed = lax.psum_scatter(
        layer_terms.astype(jnp.bfloat16), "col", scatter_dimension=1, tiled=True
    ).astype(jnp.float32)
    layer_out = (hidden.astype(jnp.float32) + summed).astype(jnp.bfloat16)
    return (attended, layer_out)


def solution(mesh):
    small = mesh.shape["row"] == ROWS and mesh.shape["col"] == COLS
    return jax.shard_map(
        fused_body if small else gathered_body,
        mesh=mesh,
        in_specs=(
            P("row", "col"),
            P("row", "col"),
            P("row", "col"),
            P("col"),
            P(),
            P("row", "col"),
            P("col", "row"),
            P("col"),
            P("row", "col"),
            P("row", "col"),
            P("col", "row"),
            P(),
            P("row", None, "col"),
            P("row", None, "col"),
            P("row", "col", None),
            P("row", None),
            P("row", None),
        ),
        out_specs=(P("row", "col"), P("row", "col")),
        check_vma=False,
    )
```

```python
import math

import jax
import jax.numpy as jnp
from jax import lax
from jax.experimental import pallas as pl
from jax.experimental.pallas import tpu as pltpu
from jax.sharding import PartitionSpec as P

HDIM = 128
WINDOW = 4096


norm_eps = 1e-06
masked_score = -1e30


def lower_bounds(lengths, positions):
    doc_ends = jnp.cumsum(lengths)
    starts = doc_ends - lengths
    begun_docs = starts[None, :] <= positions[:, None]
    doc_start = jnp.max(jnp.where(begun_docs, starts[None, :], 0), axis=1)
    return jnp.maximum(doc_start, positions - WINDOW + 1)


MESH = pl.DeviceIdType.MESH
LONGEST = 576
ROWS = 8
COLS = 4
TOK = 128
WIDTH = 2048
PART = WIDTH // COLS
SLICE = WIDTH // ROWS
UNITS = 96
REACH = (LONGEST - 2 + TOK) // TOK
HOPS = REACH // 2
NT = (((1,), (1,)), ((), ()))


def mm(a, b):
    return jnp.dot(a, b, preferred_element_type=jnp.float32)


def layer_kernel(
    q_ref,
    k_ref,
    v_ref,
    sink_ref,
    lengths_ref,
    stream_ref,
    wo_ref,
    gain_ref,
    sh_ref,
    switch_ref,
    eg_hbm,
    eu_hbm,
    ed_hbm,
    routes_ref,
    route_weights_ref,
    att_ref,
    out_ref,
    eg_ref,
    eu_ref,
    ed_ref,
    gain_send,
    switch_buf,
    w_send,
    kv_buf,
    wo_buf,
    gain_buf,
    sh_buf,
    w_buf,
    head_send,
    head_recv,
    hid,
    own_hidden,
    keep_a,
    keep_b,
    send1,
    recv1,
    send2,
    recv2,
    send3,
    recv3,
    send4,
    recv4,
    s_local,
    s_kv,
    r_kv,
    s_wo,
    r_wo,
    s_gain,
    r_gain,
    s_sh,
    r_sh,
    s_w,
    r_w,
    s_head,
    r_head,
    s_row,
    r_row,
    s_pass,
    s_core,
    r_core,
    s_x,
    r_x,
    s_fwd,
    r_fwd,
    s_1,
    r_1,
    s_2,
    r_2,
    s_3,
    r_3,
    s_4,
    r_4,
):
    r = lax.axis_index("row")
    c = lax.axis_index("col")
    core_peer = c + 1 - 2 * (c % 2)
    x_peer = (c + 2) % COLS
    far_peer = (core_peer + 2) % COLS
    depth = ROWS // 2
    z = r // 2
    y = r % 2
    partner = r + 1 - 2 * y

    def ahead(d):
        return ((z + d) % depth) * 2 + y

    def origin(t):
        return ((z + depth - t // 2) % depth) * 2 + (y + t % 2) % 2

    def up(k):
        return (r + k) % ROWS

    def down(k):
        return (r + ROWS - k) % ROWS

    def cols(i, n):
        return pl.ds(pl.multiple_of(i * n, n), n)

    locals_ = [
        pltpu.make_async_copy(a, b, s_local.at[i])
        for i, (a, b) in enumerate(((eg_hbm, eg_ref), (eu_hbm, eu_ref), (ed_hbm, ed_ref)))
    ]
    for copy in locals_:
        copy.start()

    barrier = pltpu.get_barrier_semaphore()
    for k in range(1, ROWS):
        pl.semaphore_signal(barrier, inc=1, device_id=(up(k), c), device_id_type=MESH)
    for k in range(1, COLS):
        pl.semaphore_signal(barrier, inc=1, device_id=(r, (c + k) % COLS), device_id_type=MESH)
    pl.semaphore_wait(barrier, ROWS - 1 + COLS - 1)

    def push(src, dst, send, recv, where):
        return pltpu.make_async_remote_copy(
            src_ref=src,
            dst_ref=dst,
            send_sem=send,
            recv_sem=recv,
            device_id=where,
            device_id_type=MESH,
        )

    def kv_copy(i, from_slot, to_slot, sem, row):
        own = (k_ref, v_ref)[i]
        src = own if from_slot == 0 else kv_buf.at[i, pl.ds(from_slot * TOK, TOK)]
        dst = kv_buf.at[i, cols(to_slot, TOK)]
        return push(src, dst, s_kv.at[i, sem], r_kv.at[i, to_slot], (row, c))

    def wo_copy(t, sem, row):
        piece = wo_buf.at[:, cols(origin(t), SLICE)]
        return push(piece, piece, s_wo.at[sem], r_wo.at[t], (row, c))

    def wo_send(sem, t, row):
        return push(wo_ref, wo_buf.at[:, cols(r, SLICE)], s_wo.at[sem], r_wo.at[t], (row, c))

    def wo_pass(d):
        piece = wo_buf.at[:, cols(origin(2 * d), SLICE)]
        return push(piece, piece, s_wo.at[depth + d], r_wo.at[2 * d + 1], (partner, c))

    def sh_copy(k, block):
        return push(
            sh_ref.at[up(k)],
            sh_buf.at[:, :, cols(block, SLICE)],
            s_sh.at[k],
            r_sh.at[k],
            (up(k), c),
        )

    def w_copy(k):
        return push(w_send.at[up(k)], w_buf.at[k], s_w.at[k], r_w.at[k], (up(k), c))

    def gain_copy(k, block):
        return push(
            gain_send,
            gain_buf.at[:, cols(block, PART)],
            s_gain.at[k],
            r_gain.at[k],
            (r, (c + k) % COLS),
        )

    def head_copy(k):
        return push(
            head_send.at[k], head_recv.at[k], s_head.at[k], r_head.at[k], (r, (c + k) % COLS)
        )

    def both(fn, *args):
        for i in range(2):
            getattr(kv_copy(i, *args), fn)()

    near = 2 * HOPS

    def sends(fn):
        for d in range(1, HOPS + 1):

            @pl.when(z + d < depth)
            def _():
                both(fn, 0, 2 * d, d, jnp.minimum(r + 2 * d, ROWS - 1))

        @pl.when(y == 0)
        def _():
            both(fn, 0, 1, 0, partner)

        @pl.when(r == 1)
        def _():
            both(fn, 0, REACH, near + 1, r + REACH)

    def handovers(fn):
        for d in range(1, HOPS + 1):

            @pl.when(z >= d)
            def _():
                both(fn, 2 * d, 2 * d + 1 - 2 * y, HOPS + d, partner)

    def arrived(k):
        @pl.when(r >= k)
        def _():
            both("wait_recv", 0, k, 0, partner)

    sends("start")
    for d in range(1, depth):
        wo_send(d, 2 * d, ahead(d)).start()
    wo_send(depth, 1, partner).start()

    for i in range(PART // HDIM):
        gain_send[:, i * HDIM : (i + 1) * HDIM] = jnp.broadcast_to(
            gain_ref[i : i + 1, :].astype(jnp.float32), (8, HDIM)
        )
    for e in range(ROWS):
        picked = jnp.where(routes_ref[...] == e, route_weights_ref[...], 0.0)
        w_send[e] = jnp.broadcast_to(jnp.sum(picked, axis=0, keepdims=True), (8, TOK))
    for k in range(1, COLS):
        gain_copy(k, c).start()
    for k in range(1, ROWS):
        w_copy(k).start()

    kv_buf[0, 0:TOK] = k_ref[...]
    kv_buf[1, 0:TOK] = v_ref[...]
    wo_buf[:, cols(r, SLICE)] = wo_ref[...]
    gain_buf[:, cols(c, PART)] = gain_send[...]
    sh_buf[:, :, cols(r, SLICE)] = sh_ref[r]
    w_buf[0] = w_send[r]
    for i in range(WIDTH // HDIM):
        switch_buf[:, i * HDIM : (i + 1) * HDIM] = jnp.broadcast_to(
            switch_ref[i : i + 1, :].astype(jnp.float32), (8, HDIM)
        )

    for k in range(1, REACH + 1):

        @pl.when(r < k)
        def _():
            kv_buf[:, k * TOK : (k + 1) * TOK] = jnp.zeros((2, TOK, 2 * HDIM), jnp.bfloat16)

    for d in range(1, HOPS + 1):
        arrived(2 * d)
    handovers("start")
    for d in range(1, depth - 1):
        wo_copy(2 * d, 0, partner).wait_recv()
        wo_pass(d).start()
    for k in range(1, REACH + 1, 2):
        arrived(k)

    keys = (REACH + 1) * TOK
    place = lax.broadcasted_iota(jnp.int32, (TOK, keys), 1)
    key_place = (r - place // TOK) * TOK + place % TOK
    rows_at = r * TOK + lax.broadcasted_iota(jnp.int32, (TOK, 1), 0)
    lower = jnp.maximum(rows_at - WINDOW + 1, 0)
    begin = jnp.int32(0)
    for d in range(lengths_ref.shape[0]):
        lower = jnp.maximum(lower, jnp.where(rows_at >= begin, begin, 0))
        begin = begin + lengths_ref[d]
    visible = (key_place >= lower) & (key_place <= rows_at)
    for h in range(2):
        lanes = slice(h * HDIM, (h + 1) * HDIM)
        scores = lax.dot_general(
            q_ref[:, lanes], kv_buf[0, :, lanes], NT, preferred_element_type=jnp.float32
        ) * (1.0 / math.sqrt(HDIM))
        masked = jnp.where(visible, scores, masked_score)
        sink = sink_ref[h]
        row_max = jnp.maximum(jnp.max(masked, axis=1, keepdims=True), sink)
        weight = jnp.where(visible, jnp.exp(masked - row_max), 0.0)
        denominator = jnp.exp(sink - row_max) + jnp.sum(weight, axis=1, keepdims=True)
        mixture = mm(weight.astype(jnp.bfloat16), kv_buf[1, :, lanes])
        att_ref[:, lanes] = (mixture / denominator).astype(jnp.bfloat16)
        if h == 0:
            wo_copy(2 * depth - 2, 0, partner).wait_recv()
            wo_pass(depth - 1).start()
            for k in range(1, ROWS):
                sh_copy(k, r).start()

    for d in range(depth):
        wo_copy(2 * d + 1, 0, partner).wait_recv()
    attended = att_ref[...]
    for k in range(1, COLS):
        head_send[k] = mm(attended, wo_buf[:, cols((c + k) % COLS, PART)]).astype(jnp.bfloat16)
        head_copy(k).start()
    total = stream_ref[...].astype(jnp.float32) + mm(attended, wo_buf[:, cols(c, PART)])
    for k in range(1, COLS):
        head_copy(k).wait_recv()
        total = total + head_recv[k].astype(jnp.float32)
    hidden = total.astype(jnp.bfloat16)
    own_hidden[...] = hidden
    hid[cols(r, TOK), cols(c, PART)] = hidden

    def row_copy(d):
        return push(
            own_hidden,
            hid.at[cols(r, TOK), cols(c, PART)],
            s_row.at[d],
            r_row.at[2 * d],
            (ahead(d), c),
        )

    def pass_copy(t, arrival):
        piece = hid.at[cols(origin(t), TOK), cols(c, PART)]
        return push(piece, piece, s_pass.at[t], r_row.at[arrival], (partner, c))

    def side_copy(k, col, send, recv, peer):
        piece = hid.at[cols(origin(k), TOK), cols(col, PART)]
        return push(piece, piece, send.at[k], recv.at[k], (r, peer))

    def copy1(k):
        return push(send1.at[k], recv1.at[k], s_1.at[k], r_1.at[k], (r, core_peer))

    def copy2(k):
        return push(send2.at[k], recv2.at[k], s_2.at[k], r_2.at[k], (r, x_peer))

    def copy3(t):
        return push(send3.at[t], recv3.at[t // 2], s_3.at[t], r_3.at[t // 2], (partner, c))

    def copy4(d):
        return push(send4.at[d], recv4.at[d], s_4.at[d], r_4.at[d], (origin(2 * d), c))

    for d in range(1, depth):
        row_copy(d).start()

    for k in range(1, ROWS):
        sh_copy(k, down(k)).wait_recv()
        w_copy(k).wait_recv()
    for k in range(1, COLS):
        gain_copy(k, (c + COLS - k) % COLS).wait_recv()
    for copy in locals_:
        copy.wait()

    def experts(k):
        row = origin(k)
        widened = hid[cols(row, TOK), :].astype(jnp.float32)
        mean = jnp.mean(widened * widened, axis=1, keepdims=True)
        normed = (widened * lax.rsqrt(mean + norm_eps) * gain_buf[0:1, :]).astype(jnp.bfloat16)
        logit = jnp.sum(normed.astype(jnp.float32) * switch_buf[0:1, :], axis=1, keepdims=True)
        switch = 1.0 / (1.0 + jnp.exp(-logit))
        weights = jnp.broadcast_to(w_buf[(r + ROWS - row) % ROWS, 0:1, :], (TOK, TOK)).T[:, 0:1]
        gate = lax.dot_general(normed, eg_ref[...], NT, preferred_element_type=jnp.float32)
        raised = lax.dot_general(normed, eu_ref[...], NT, preferred_element_type=jnp.float32)
        act = gate / (1.0 + jnp.exp(-gate)) * raised
        act = (act * weights).astype(jnp.bfloat16)
        gate = lax.dot_general(normed, sh_buf[0], NT, preferred_element_type=jnp.float32)
        raised = lax.dot_general(normed, sh_buf[1], NT, preferred_element_type=jnp.float32)
        shared = (gate / (1.0 + jnp.exp(-gate)) * raised * switch).astype(jnp.bfloat16)

        def term(col):
            lanes = cols(col, PART)
            return mm(act, ed_ref[:, lanes]) + mm(shared, sh_buf[2, :, lanes])

        send1[k, 0] = term(core_peer).astype(jnp.bfloat16)
        send1[k, 1] = term(far_peer).astype(jnp.bfloat16)
        copy1(k).start()
        keep_b[k] = term(x_peer)
        keep_a[k] = term(c)

    def step(s, carry):
        @pl.when(s < ROWS)
        def _():
            @pl.when(s > 0)
            def _():
                pass_copy(s, s).wait_recv()

            @pl.when(s % 2 == 0)
            def _():
                pass_copy(s, s + 1).start()

            side_copy(s, c, s_core, r_core, core_peer).start()
            side_copy(s, c, s_x, r_x, x_peer).start()

        @pl.when((s >= 1) & (s < ROWS + 1))
        def _():
            side_copy(s - 1, x_peer, s_x, r_x, x_peer).wait_recv()
            side_copy(s - 1, x_peer, s_fwd, r_fwd, core_peer).start()

        @pl.when((s >= 2) & (s < ROWS + 2))
        def _():
            side_copy(s - 2, core_peer, s_core, r_core, core_peer).wait_recv()
            side_copy(s - 2, far_peer, s_fwd, r_fwd, core_peer).wait_recv()
            experts(s - 2)

        @pl.when((s >= 3) & (s < ROWS + 3))
        def _():
            k = s - 3
            copy1(k).wait_recv()
            send2[k] = (keep_b[k] + recv1[k, 1].astype(jnp.float32)).astype(jnp.bfloat16)
            copy2(k).start()
            keep_a[k] = keep_a[k] + recv1[k, 0].astype(jnp.float32)

        @pl.when((s >= 4) & (s < ROWS + 4))
        def _():
            k = s - 4
            copy2(k).wait_recv()
            done = keep_a[k] + recv2[k].astype(jnp.float32)
            keep_a[k] = done

            @pl.when(k % 2 == 1)
            def _():
                send3[k] = done.astype(jnp.bfloat16)
                copy3(k).start()

        @pl.when((s >= 6) & (s % 2 == 0))
        def _():
            d = (s - 6) // 2
            copy3(2 * d + 1).wait_recv()
            done = keep_a[2 * d] + recv3[d].astype(jnp.float32)
            keep_a[2 * d] = done

            @pl.when(d > 0)
            def _():
                send4[d] = done.astype(jnp.bfloat16)
                copy4(d).start()

        return carry

    lax.fori_loop(0, ROWS + 5, step, 0)

    total = own_hidden[...].astype(jnp.float32) + keep_a[0]
    for d in range(1, depth):
        copy4(d).wait_recv()
        total = total + recv4[d].astype(jnp.float32)
    out_ref[...] = total.astype(jnp.bfloat16)

    sends("wait_send")
    handovers("wait_send")
    for d in range(1, depth):
        wo_send(d, 2 * d, ahead(d)).wait_send()
        wo_pass(d).wait_send()
        row_copy(d).wait_send()
        copy4(d).wait_send()
    wo_send(depth, 1, partner).wait_send()

    for k in range(1, COLS):
        gain_copy(k, c).wait_send()
        head_copy(k).wait_send()
    for k in range(ROWS):
        if k > 0:
            w_copy(k).wait_send()
            sh_copy(k, r).wait_send()
        if k % 2 == 0:
            pass_copy(k, k + 1).wait_send()
        else:
            copy3(k).wait_send()
        side_copy(k, c, s_core, r_core, core_peer).wait_send()
        side_copy(k, c, s_x, r_x, x_peer).wait_send()
        side_copy(k, x_peer, s_fwd, r_fwd, core_peer).wait_send()
        copy1(k).wait_send()
        copy2(k).wait_send()


def fused_body(
    queries,
    key_vectors,
    values,
    sink_logit,
    lengths,
    stream,
    out_weight,
    norm_gain,
    shared_gate,
    shared_up,
    shared_down,
    shared_switch,
    expert_gate,
    expert_up,
    expert_down,
    routes,
    route_weights,
):
    units = shared_gate.shape[1] // ROWS
    shared = jnp.stack(
        [
            shared_gate.T.reshape(ROWS, units, SLICE),
            shared_up.T.reshape(ROWS, units, SLICE),
            shared_down.reshape(ROWS, units, SLICE),
        ],
        1,
    )
    shared = jnp.pad(shared, ((0, 0), (0, 0), (0, UNITS - units), (0, 0)))
    bf16, f32 = jnp.bfloat16, jnp.float32
    eight = pltpu.SemaphoreType.DMA((ROWS,))
    four = pltpu.SemaphoreType.DMA((COLS,))
    pair = pltpu.SemaphoreType.DMA((2, ROWS))
    vmem = pl.BlockSpec(memory_space=pltpu.VMEM)
    smem = pl.BlockSpec(memory_space=pltpu.SMEM)
    hbm = pl.BlockSpec(memory_space=pl.ANY)
    hidden_units = expert_down.shape[1]
    return pl.pallas_call(
        layer_kernel,
        out_shape=(
            jax.ShapeDtypeStruct(queries.shape, bf16),
            jax.ShapeDtypeStruct(stream.shape, bf16),
        ),
        in_specs=[vmem] * 3 + [smem] * 2 + [vmem] * 5 + [hbm] * 3 + [vmem] * 2,
        out_specs=(vmem, vmem),
        scratch_shapes=[
            pltpu.VMEM((hidden_units, WIDTH), bf16),
            pltpu.VMEM((hidden_units, WIDTH), bf16),
            pltpu.VMEM((hidden_units, WIDTH), bf16),
            pltpu.VMEM((8, PART), f32),
            pltpu.VMEM((8, WIDTH), f32),
            pltpu.VMEM((ROWS, 8, TOK), f32),
            pltpu.VMEM((2, (REACH + 1) * TOK, 2 * HDIM), bf16),
            pltpu.VMEM((2 * HDIM, WIDTH), bf16),
            pltpu.VMEM((8, WIDTH), f32),
            pltpu.VMEM((3, UNITS, WIDTH), bf16),
            pltpu.VMEM((ROWS, 8, TOK), f32),
            pltpu.VMEM((COLS, TOK, PART), bf16),
            pltpu.VMEM((COLS, TOK, PART), bf16),
            pltpu.VMEM((ROWS * TOK, WIDTH), bf16),
            pltpu.VMEM((TOK, PART), bf16),
            pltpu.VMEM((ROWS, TOK, PART), f32),
            pltpu.VMEM((ROWS, TOK, PART), f32),
            pltpu.VMEM((ROWS, 2, TOK, PART), bf16),
            pltpu.VMEM((ROWS, 2, TOK, PART), bf16),
            pltpu.VMEM((ROWS, TOK, PART), bf16),
            pltpu.VMEM((ROWS, TOK, PART), bf16),
            pltpu.VMEM((ROWS, TOK, PART), bf16),
            pltpu.VMEM((COLS, TOK, PART), bf16),
            pltpu.VMEM((COLS, TOK, PART), bf16),
            pltpu.VMEM((COLS, TOK, PART), bf16),
            pltpu.SemaphoreType.DMA((3,)),
            pair,
            pair,
            eight,
            eight,
            four,
            four,
            eight,
            eight,
            eight,
            eight,
            four,
            four,
        ]
        + [eight] * 17,
        compiler_params=pltpu.CompilerParams(
            collective_id=0, has_side_effects=True, vmem_limit_bytes=58 << 20
        ),
    )(
        queries,
        key_vectors,
        values,
        sink_logit,
        lengths,
        stream,
        out_weight,
        norm_gain.reshape(PART // HDIM, HDIM),
        shared,
        shared_switch.reshape(WIDTH // HDIM, HDIM),
        expert_gate[0].T,
        expert_up[0].T,
        expert_down[0],
        routes.T,
        route_weights.T,
    )


def gathered_body(
    queries,
    key_vectors,
    values,
    sink_logit,
    lengths,
    stream,
    out_weight,
    norm_gain,
    shared_gate,
    shared_up,
    shared_down,
    shared_switch,
    expert_gate,
    expert_up,
    expert_down,
    routes,
    route_weights,
):
    local_tokens = queries.shape[0]
    feature_width = queries.shape[1]
    head_count = feature_width // HDIM
    my_row = lax.axis_index("row")
    positions = my_row * local_tokens + jnp.arange(local_tokens, dtype=jnp.int32)
    lower_bound = lower_bounds(lengths, positions)
    query_heads = queries.reshape(local_tokens, head_count, HDIM)
    score_scale = 1.0 / math.sqrt(HDIM)
    key_value = jnp.stack([key_vectors, values], 0)
    key_piece = lax.all_gather(key_value, "row", axis=1, tiled=True)
    row_max = jnp.broadcast_to(sink_logit[None, :], (local_tokens, head_count))
    denominator = jnp.ones((local_tokens, head_count), jnp.float32)
    numerator = jnp.zeros((local_tokens, head_count, HDIM), jnp.float32)
    needed = key_piece.shape[1]
    key_heads = key_piece[0].reshape(needed, head_count, HDIM)
    value_heads = key_piece[1].reshape(needed, head_count, HDIM)
    scores = (
        jnp.einsum("qhd,khd->qhk", query_heads, key_heads, preferred_element_type=jnp.float32)
        * score_scale
    )
    key_places = jnp.arange(needed, dtype=jnp.int32)
    visible = (
        (key_places[None, :] >= lower_bound[:, None]) & (key_places[None, :] <= positions[:, None])
    )[:, None, :]
    masked = jnp.where(visible, scores, masked_score)
    new_max = jnp.maximum(row_max, jnp.max(masked, axis=2))
    weight = jnp.where(visible, jnp.exp(masked - new_max[:, :, None]), 0.0)
    rescale = jnp.exp(row_max - new_max)
    denominator = denominator * rescale + jnp.sum(weight, axis=2)
    numerator = numerator * rescale[:, :, None] + jnp.einsum(
        "qhk,khd->qhd", weight.astype(jnp.bfloat16), value_heads, preferred_element_type=jnp.float32
    )
    final_max, denominator, numerator = (new_max, denominator, numerator)
    attended = (
        (numerator / denominator[:, :, None])
        .reshape(local_tokens, feature_width)
        .astype(jnp.bfloat16)
    )
    head_terms = jnp.dot(
        attended,
        lax.all_gather(out_weight, "row", axis=1, tiled=True),
        preferred_element_type=jnp.float32,
    )
    mixed_heads = lax.psum_scatter(
        head_terms.astype(jnp.bfloat16), "col", scatter_dimension=1, tiled=True
    ).astype(jnp.float32)
    hidden = (stream.astype(jnp.float32) + mixed_heads).astype(jnp.bfloat16)
    widened = hidden.astype(jnp.float32)
    full_width = lax.axis_size("col") * hidden.shape[1]
    squares = lax.psum(jnp.sum(widened * widened, axis=1), "col")
    row_scale = lax.rsqrt(squares / full_width + norm_eps)
    normed_part = (widened * row_scale[:, None] * norm_gain.astype(jnp.float32)).astype(
        jnp.bfloat16
    )
    normed = lax.all_gather(normed_part, "col", axis=1, tiled=True)
    gate_part = jnp.dot(
        normed,
        lax.all_gather(shared_gate, "row", axis=0, tiled=True),
        preferred_element_type=jnp.float32,
    )
    up_part = jnp.dot(
        normed,
        lax.all_gather(shared_up, "row", axis=0, tiled=True),
        preferred_element_type=jnp.float32,
    )
    shared_act = (jax.nn.silu(gate_part) * up_part).astype(jnp.bfloat16)
    shared_part = jnp.dot(
        shared_act,
        lax.all_gather(shared_down, "row", axis=1, tiled=True),
        preferred_element_type=jnp.float32,
    )
    switch = jax.nn.sigmoid(jnp.dot(normed, shared_switch, preferred_element_type=jnp.float32))
    row_count = lax.axis_size("row")
    fanout = routes.shape[1]
    model_width = normed.shape[1]
    capacity = max(2, min(local_tokens, 3 * local_tokens * fanout // (2 * row_count)))
    flat_routes = routes.reshape(-1)
    onehot = (flat_routes[:, None] == jnp.arange(row_count, dtype=jnp.int32)[None, :]).astype(
        jnp.int32
    )
    before = jnp.cumsum(onehot, axis=0) - onehot
    slot_index = jnp.sum(before * onehot, axis=1)
    target = flat_routes * capacity + slot_index
    owner_row = jnp.arange(local_tokens * fanout, dtype=jnp.int32) // fanout
    source = jnp.full((row_count * capacity,), local_tokens, jnp.int32).at[target].set(owner_row)
    padded = jnp.concatenate([normed, jnp.zeros((1, model_width), jnp.bfloat16)], 0)
    outgoing = padded[source].reshape(row_count, capacity, model_width)
    received = lax.all_to_all(outgoing, "row", split_axis=0, concat_axis=0, tiled=True)
    senders, slot_count, received_width = received.shape
    dispatched = received.reshape(senders * slot_count, received_width)
    gate_out = jnp.dot(dispatched, expert_gate[0], preferred_element_type=jnp.float32)
    up_out = jnp.dot(dispatched, expert_up[0], preferred_element_type=jnp.float32)
    activation = (jax.nn.silu(gate_out) * up_out).astype(jnp.bfloat16)
    partial_out = jnp.dot(activation, expert_down[0], preferred_element_type=jnp.float32).astype(
        jnp.bfloat16
    )
    returned = lax.all_to_all(
        partial_out.reshape(senders, slot_count, received_width),
        "row",
        split_axis=0,
        concat_axis=0,
        tiled=True,
    )
    route_rows = returned.reshape(row_count * capacity, model_width)[target].reshape(
        local_tokens, fanout, model_width
    )
    routed = jnp.zeros((local_tokens, model_width), jnp.float32)
    for route_slot in range(fanout):
        routed = routed + route_weights[:, route_slot][:, None] * route_rows[
            :, route_slot, :
        ].astype(jnp.float32)
    layer_terms = switch[:, None] * shared_part + routed
    summed = lax.psum_scatter(
        layer_terms.astype(jnp.bfloat16), "col", scatter_dimension=1, tiled=True
    ).astype(jnp.float32)
    layer_out = (hidden.astype(jnp.float32) + summed).astype(jnp.bfloat16)
    return (attended, layer_out)


def solution(mesh):
    small = mesh.shape["row"] == ROWS and mesh.shape["col"] == COLS
    return jax.shard_map(
        fused_body if small else gathered_body,
        mesh=mesh,
        in_specs=(
            P("row", "col"),
            P("row", "col"),
            P("row", "col"),
            P("col"),
            P(),
            P("row", "col"),
            P("col", "row"),
            P("col"),
            P("row", "col"),
            P("row", "col"),
            P("col", "row"),
            P(),
            P("row", None, "col"),
            P("row", None, "col"),
            P("row", "col", None),
            P("row", None),
            P("row", None),
        ),
        out_specs=(P("row", "col"), P("row", "col")),
        check_vma=False,
    )
```

```python
import math

import jax
import jax.numpy as jnp
from jax import lax
from jax.experimental import pallas as pl
from jax.experimental.pallas import tpu as pltpu
from jax.sharding import PartitionSpec as P

HDIM = 128
WINDOW = 4096


norm_eps = 1e-06
masked_score = -1e30


def lower_bounds(lengths, positions):
    doc_ends = jnp.cumsum(lengths)
    starts = doc_ends - lengths
    begun_docs = starts[None, :] <= positions[:, None]
    doc_start = jnp.max(jnp.where(begun_docs, starts[None, :], 0), axis=1)
    return jnp.maximum(doc_start, positions - WINDOW + 1)


MESH = pl.DeviceIdType.MESH
LONGEST = 576
ROWS = 8
COLS = 4
TOK = 128
WIDTH = 2048
PART = WIDTH // COLS
SLICE = WIDTH // ROWS
UNITS = 96
REACH = (LONGEST - 2 + TOK) // TOK
HOPS = REACH // 2
NT = (((1,), (1,)), ((), ()))


def mm(a, b):
    return jnp.dot(a, b, preferred_element_type=jnp.float32)


def layer_kernel(
    q_ref,
    k_ref,
    v_ref,
    sink_ref,
    lengths_ref,
    stream_ref,
    wo_ref,
    gain_ref,
    sh_ref,
    switch_ref,
    eg_hbm,
    eu_hbm,
    ed_hbm,
    routes_ref,
    route_weights_ref,
    att_ref,
    out_ref,
    weights,
    gain_send,
    switch_buf,
    w_send,
    kv_buf,
    wo_buf,
    gain_buf,
    w_buf,
    head_send,
    head_recv,
    hid,
    own_hidden,
    keep_a,
    keep_b,
    send1,
    recv1,
    send2,
    recv2,
    send3,
    recv3,
    send4,
    recv4,
    s_local,
    s_kv,
    r_kv,
    s_wo,
    r_wo,
    s_gain,
    r_gain,
    s_sh,
    r_sh,
    s_w,
    r_w,
    s_head,
    r_head,
    s_row,
    r_row,
    s_pass,
    s_core,
    r_core,
    s_x,
    r_x,
    s_fwd,
    r_fwd,
    s_1,
    r_1,
    s_2,
    r_2,
    s_3,
    r_3,
    s_4,
    r_4,
):
    r = lax.axis_index("row")
    c = lax.axis_index("col")
    core_peer = c + 1 - 2 * (c % 2)
    x_peer = (c + 2) % COLS
    far_peer = (core_peer + 2) % COLS
    depth = ROWS // 2
    z = r // 2
    y = r % 2
    partner = r + 1 - 2 * y

    def ahead(d):
        return ((z + d) % depth) * 2 + y

    def origin(t):
        return ((z + depth - t // 2) % depth) * 2 + (y + t % 2) % 2

    def up(k):
        return (r + k) % ROWS

    def down(k):
        return (r + ROWS - k) % ROWS

    def cols(i, n):
        return pl.ds(pl.multiple_of(i * n, n), n)

    routed_units = eg_hbm.shape[0]
    own_units = weights.at[:, 0:routed_units]
    sh_buf = weights.at[:, routed_units : routed_units + UNITS]
    locals_ = [
        pltpu.make_async_copy(a, b, s_local.at[i])
        for i, (a, b) in enumerate(((eg_hbm, own_units.at[0]), (eu_hbm, own_units.at[1]), (ed_hbm, own_units.at[2])))
    ]
    for copy in locals_:
        copy.start()

    barrier = pltpu.get_barrier_semaphore()
    for k in range(1, ROWS):
        pl.semaphore_signal(barrier, inc=1, device_id=(up(k), c), device_id_type=MESH)
    for k in range(1, COLS):
        pl.semaphore_signal(barrier, inc=1, device_id=(r, (c + k) % COLS), device_id_type=MESH)
    pl.semaphore_wait(barrier, ROWS - 1 + COLS - 1)

    def push(src, dst, send, recv, where):
        return pltpu.make_async_remote_copy(
            src_ref=src,
            dst_ref=dst,
            send_sem=send,
            recv_sem=recv,
            device_id=where,
            device_id_type=MESH,
        )

    def kv_copy(i, from_slot, to_slot, sem, row):
        own = (k_ref, v_ref)[i]
        src = own if from_slot == 0 else kv_buf.at[i, pl.ds(from_slot * TOK, TOK)]
        dst = kv_buf.at[i, cols(to_slot, TOK)]
        return push(src, dst, s_kv.at[i, sem], r_kv.at[i, to_slot], (row, c))

    def wo_copy(t, sem, row):
        piece = wo_buf.at[:, cols(origin(t), SLICE)]
        return push(piece, piece, s_wo.at[sem], r_wo.at[t], (row, c))

    def wo_send(sem, t, row):
        return push(wo_ref, wo_buf.at[:, cols(r, SLICE)], s_wo.at[sem], r_wo.at[t], (row, c))

    def wo_pass(d):
        piece = wo_buf.at[:, cols(origin(2 * d), SLICE)]
        return push(piece, piece, s_wo.at[depth + d], r_wo.at[2 * d + 1], (partner, c))

    def sh_copy(k, block):
        return push(
            sh_ref.at[up(k)],
            sh_buf.at[:, :, cols(block, SLICE)],
            s_sh.at[k],
            r_sh.at[k],
            (up(k), c),
        )

    def w_copy(k):
        return push(w_send.at[up(k)], w_buf.at[k], s_w.at[k], r_w.at[k], (up(k), c))

    def gain_copy(k, block):
        return push(
            gain_send,
            gain_buf.at[:, cols(block, PART)],
            s_gain.at[k],
            r_gain.at[k],
            (r, (c + k) % COLS),
        )

    def head_copy(k):
        return push(
            head_send.at[k], head_recv.at[k], s_head.at[k], r_head.at[k], (r, (c + k) % COLS)
        )

    def both(fn, *args):
        for i in range(2):
            getattr(kv_copy(i, *args), fn)()

    near = 2 * HOPS

    def sends(fn):
        for d in range(1, HOPS + 1):

            @pl.when(z + d < depth)
            def _():
                both(fn, 0, 2 * d, d, jnp.minimum(r + 2 * d, ROWS - 1))

        @pl.when(y == 0)
        def _():
            both(fn, 0, 1, 0, partner)

        @pl.when(r == 1)
        def _():
            both(fn, 0, REACH, near + 1, r + REACH)

    def handovers(fn):
        for d in range(1, HOPS + 1):

            @pl.when(z >= d)
            def _():
                both(fn, 2 * d, 2 * d + 1 - 2 * y, HOPS + d, partner)

    def arrived(k):
        @pl.when(r >= k)
        def _():
            both("wait_recv", 0, k, 0, partner)

    sends("start")
    for d in range(1, depth):
        wo_send(d, 2 * d, ahead(d)).start()
    wo_send(depth, 1, partner).start()

    for i in range(PART // HDIM):
        gain_send[:, i * HDIM : (i + 1) * HDIM] = jnp.broadcast_to(
            gain_ref[i : i + 1, :].astype(jnp.float32), (8, HDIM)
        )
    for e in range(ROWS):
        picked = jnp.where(routes_ref[...] == e, route_weights_ref[...], 0.0)
        w_send[e] = jnp.broadcast_to(jnp.sum(picked, axis=0, keepdims=True), (8, TOK))
    for k in range(1, COLS):
        gain_copy(k, c).start()
    for k in range(1, ROWS):
        w_copy(k).start()

    kv_buf[0, 0:TOK] = k_ref[...]
    kv_buf[1, 0:TOK] = v_ref[...]
    wo_buf[:, cols(r, SLICE)] = wo_ref[...]
    gain_buf[:, cols(c, PART)] = gain_send[...]
    sh_buf[:, :, cols(r, SLICE)] = sh_ref[r]
    w_buf[0] = w_send[r]
    for i in range(WIDTH // HDIM):
        switch_buf[:, i * HDIM : (i + 1) * HDIM] = jnp.broadcast_to(
            switch_ref[i : i + 1, :].astype(jnp.float32), (8, HDIM)
        )

    for k in range(1, REACH + 1):

        @pl.when(r < k)
        def _():
            kv_buf[:, k * TOK : (k + 1) * TOK] = jnp.zeros((2, TOK, 2 * HDIM), jnp.bfloat16)

    for d in range(1, HOPS + 1):
        arrived(2 * d)
    handovers("start")
    for d in range(1, depth - 1):
        wo_copy(2 * d, 0, partner).wait_recv()
        wo_pass(d).start()
    for k in range(1, REACH + 1, 2):
        arrived(k)

    keys = (REACH + 1) * TOK
    place = lax.broadcasted_iota(jnp.int32, (TOK, keys), 1)
    key_place = (r - place // TOK) * TOK + place % TOK
    rows_at = r * TOK + lax.broadcasted_iota(jnp.int32, (TOK, 1), 0)
    lower = jnp.maximum(rows_at - WINDOW + 1, 0)
    begin = jnp.int32(0)
    for d in range(lengths_ref.shape[0]):
        lower = jnp.maximum(lower, jnp.where(rows_at >= begin, begin, 0))
        begin = begin + lengths_ref[d]
    visible = (key_place >= lower) & (key_place <= rows_at)
    for h in range(2):
        lanes = slice(h * HDIM, (h + 1) * HDIM)
        scores = lax.dot_general(
            q_ref[:, lanes], kv_buf[0, :, lanes], NT, preferred_element_type=jnp.float32
        ) * (1.0 / math.sqrt(HDIM))
        masked = jnp.where(visible, scores, masked_score)
        sink = sink_ref[h]
        row_max = jnp.maximum(jnp.max(masked, axis=1, keepdims=True), sink)
        weight = jnp.where(visible, jnp.exp(masked - row_max), 0.0)
        denominator = jnp.exp(sink - row_max) + jnp.sum(weight, axis=1, keepdims=True)
        mixture = mm(weight.astype(jnp.bfloat16), kv_buf[1, :, lanes])
        att_ref[:, lanes] = (mixture / denominator).astype(jnp.bfloat16)
        if h == 0:
            wo_copy(2 * depth - 2, 0, partner).wait_recv()
            wo_pass(depth - 1).start()
            for k in range(1, ROWS):
                sh_copy(k, r).start()

    for d in range(depth):
        wo_copy(2 * d + 1, 0, partner).wait_recv()
    attended = att_ref[...]
    for k in range(1, COLS):
        head_send[k] = mm(attended, wo_buf[:, cols((c + k) % COLS, PART)]).astype(jnp.bfloat16)
        head_copy(k).start()
    total = stream_ref[...].astype(jnp.float32) + mm(attended, wo_buf[:, cols(c, PART)])
    for k in range(1, COLS):
        head_copy(k).wait_recv()
        total = total + head_recv[k].astype(jnp.float32)
    hidden = total.astype(jnp.bfloat16)
    own_hidden[...] = hidden
    hid[cols(r, TOK), cols(c, PART)] = hidden

    def row_copy(d):
        return push(
            own_hidden,
            hid.at[cols(r, TOK), cols(c, PART)],
            s_row.at[d],
            r_row.at[2 * d],
            (ahead(d), c),
        )

    def pass_copy(t, arrival):
        piece = hid.at[cols(origin(t), TOK), cols(c, PART)]
        return push(piece, piece, s_pass.at[t], r_row.at[arrival], (partner, c))

    def side_copy(k, col, send, recv, peer):
        piece = hid.at[cols(origin(k), TOK), cols(col, PART)]
        return push(piece, piece, send.at[k], recv.at[k], (r, peer))

    def cross_pass(t):
        piece = hid.at[cols(origin(t), TOK), cols(x_peer, PART)]
        return push(piece, piece, s_x.at[t + 1], r_x.at[t + 1], (partner, c))

    def copy1(k):
        return push(send1.at[k], recv1.at[k], s_1.at[k], r_1.at[k], (r, core_peer))

    def copy2(k):
        return push(send2.at[k], recv2.at[k], s_2.at[k], r_2.at[k], (r, x_peer))

    def copy3(t):
        return push(send3.at[t], recv3.at[t // 2], s_3.at[t], r_3.at[t // 2], (partner, c))

    def copy4(d):
        return push(send4.at[d], recv4.at[d], s_4.at[d], r_4.at[d], (origin(2 * d), c))

    for d in range(1, depth):
        row_copy(d).start()

    def ready():
        for k in range(1, ROWS):
            sh_copy(k, down(k)).wait_recv()
            w_copy(k).wait_recv()
        for k in range(1, COLS):
            gain_copy(k, (c + COLS - k) % COLS).wait_recv()
        for copy in locals_:
            copy.wait()

    def experts(k):
        row = origin(k)
        widened = hid[cols(row, TOK), :].astype(jnp.float32)
        mean = jnp.mean(widened * widened, axis=1, keepdims=True)
        normed = (widened * lax.rsqrt(mean + norm_eps) * gain_buf[0:1, :]).astype(jnp.bfloat16)
        logit = jnp.sum(normed.astype(jnp.float32) * switch_buf[0:1, :], axis=1, keepdims=True)
        switch = 1.0 / (1.0 + jnp.exp(-logit))
        share = jnp.broadcast_to(w_buf[(r + ROWS - row) % ROWS, 0:1, :], (TOK, TOK)).T[:, 0:1]
        gate = lax.dot_general(normed, weights[0], NT, preferred_element_type=jnp.float32)
        raised = lax.dot_general(normed, weights[1], NT, preferred_element_type=jnp.float32)
        unit = lax.broadcasted_iota(jnp.int32, gate.shape, 1)
        act = gate / (1.0 + jnp.exp(-gate)) * raised * jnp.where(unit < routed_units, share, switch)
        act = act.astype(jnp.bfloat16)

        def term(col):
            lanes = cols(col, PART)
            return mm(act, weights[2, :, lanes])

        send1[k, 0] = term(core_peer).astype(jnp.bfloat16)
        send1[k, 1] = term(far_peer).astype(jnp.bfloat16)
        copy1(k).start()
        keep_b[k] = term(x_peer)
        keep_a[k] = term(c)

    def step(s, carry):
        @pl.when(s < ROWS)
        def _():
            @pl.when(s > 0)
            def _():
                pass_copy(s, s).wait_recv()

            @pl.when(s % 2 == 0)
            def _():
                pass_copy(s, s + 1).start()
                side_copy(s, c, s_x, r_x, x_peer).start()

            side_copy(s, c, s_core, r_core, core_peer).start()

        @pl.when((s >= 1) & (s < ROWS + 1))
        def _():
            side_copy(s - 1, x_peer, s_x, r_x, x_peer).wait_recv()

            @pl.when(s % 2 == 1)
            def _():
                cross_pass(s - 1).start()

            side_copy(s - 1, x_peer, s_fwd, r_fwd, core_peer).start()

        @pl.when(s == 4)
        def _():
            ready()

        @pl.when((s >= 4) & (s < ROWS + 4))
        def _():
            k = s - 4
            side_copy(k, core_peer, s_core, r_core, core_peer).wait_recv()
            side_copy(k, far_peer, s_fwd, r_fwd, core_peer).wait_recv()
            experts(k)

        @pl.when((s >= 5) & (s < ROWS + 5))
        def _():
            k = s - 5
            copy1(k).wait_recv()
            send2[k] = (keep_b[k] + recv1[k, 1].astype(jnp.float32)).astype(jnp.bfloat16)
            copy2(k).start()
            keep_a[k] = keep_a[k] + recv1[k, 0].astype(jnp.float32)

        @pl.when((s >= 6) & (s < ROWS + 6))
        def _():
            k = s - 6
            copy2(k).wait_recv()
            done = keep_a[k] + recv2[k].astype(jnp.float32)
            keep_a[k] = done

            @pl.when(k % 2 == 1)
            def _():
                send3[k] = done.astype(jnp.bfloat16)
                copy3(k).start()

        @pl.when((s >= 8) & (s % 2 == 0))
        def _():
            d = (s - 8) // 2
            copy3(2 * d + 1).wait_recv()
            done = keep_a[2 * d] + recv3[d].astype(jnp.float32)
            keep_a[2 * d] = done

            @pl.when(d > 0)
            def _():
                send4[d] = done.astype(jnp.bfloat16)
                copy4(d).start()

        return carry

    lax.fori_loop(0, ROWS + 7, step, 0)

    total = own_hidden[...].astype(jnp.float32) + keep_a[0]
    for d in range(1, depth):
        copy4(d).wait_recv()
        total = total + recv4[d].astype(jnp.float32)
    out_ref[...] = total.astype(jnp.bfloat16)

    sends("wait_send")
    handovers("wait_send")
    for d in range(1, depth):
        wo_send(d, 2 * d, ahead(d)).wait_send()
        wo_pass(d).wait_send()
        row_copy(d).wait_send()
        copy4(d).wait_send()
    wo_send(depth, 1, partner).wait_send()

    for k in range(1, COLS):
        gain_copy(k, c).wait_send()
        head_copy(k).wait_send()
    for k in range(ROWS):
        if k > 0:
            w_copy(k).wait_send()
            sh_copy(k, r).wait_send()
        if k % 2 == 0:
            pass_copy(k, k + 1).wait_send()
            side_copy(k, c, s_x, r_x, x_peer).wait_send()
            cross_pass(k).wait_send()
        else:
            copy3(k).wait_send()
        side_copy(k, c, s_core, r_core, core_peer).wait_send()
        side_copy(k, x_peer, s_fwd, r_fwd, core_peer).wait_send()
        copy1(k).wait_send()
        copy2(k).wait_send()


def fused_body(
    queries,
    key_vectors,
    values,
    sink_logit,
    lengths,
    stream,
    out_weight,
    norm_gain,
    shared_gate,
    shared_up,
    shared_down,
    shared_switch,
    expert_gate,
    expert_up,
    expert_down,
    routes,
    route_weights,
):
    units = shared_gate.shape[1] // ROWS
    shared = jnp.stack(
        [
            shared_gate.T.reshape(ROWS, units, SLICE),
            shared_up.T.reshape(ROWS, units, SLICE),
            shared_down.reshape(ROWS, units, SLICE),
        ],
        1,
    )
    shared = jnp.pad(shared, ((0, 0), (0, 0), (0, UNITS - units), (0, 0)))
    bf16, f32 = jnp.bfloat16, jnp.float32
    eight = pltpu.SemaphoreType.DMA((ROWS,))
    four = pltpu.SemaphoreType.DMA((COLS,))
    pair = pltpu.SemaphoreType.DMA((2, ROWS))
    vmem = pl.BlockSpec(memory_space=pltpu.VMEM)
    smem = pl.BlockSpec(memory_space=pltpu.SMEM)
    hbm = pl.BlockSpec(memory_space=pltpu.HBM)
    hidden_units = expert_down.shape[1]
    return pl.pallas_call(
        layer_kernel,
        out_shape=(
            jax.ShapeDtypeStruct(queries.shape, bf16),
            jax.ShapeDtypeStruct(stream.shape, bf16),
        ),
        in_specs=[vmem] * 3 + [smem] * 2 + [vmem] * 5 + [hbm] * 3 + [vmem] * 2,
        out_specs=(vmem, vmem),
        scratch_shapes=[
            pltpu.VMEM((3, hidden_units + UNITS, WIDTH), bf16),
            pltpu.VMEM((8, PART), f32),
            pltpu.VMEM((8, WIDTH), f32),
            pltpu.VMEM((ROWS, 8, TOK), f32),
            pltpu.VMEM((2, (REACH + 1) * TOK, 2 * HDIM), bf16),
            pltpu.VMEM((2 * HDIM, WIDTH), bf16),
            pltpu.VMEM((8, WIDTH), f32),
            pltpu.VMEM((ROWS, 8, TOK), f32),
            pltpu.VMEM((COLS, TOK, PART), bf16),
            pltpu.VMEM((COLS, TOK, PART), bf16),
            pltpu.VMEM((ROWS * TOK, WIDTH), bf16),
            pltpu.VMEM((TOK, PART), bf16),
            pltpu.VMEM((ROWS, TOK, PART), f32),
            pltpu.VMEM((ROWS, TOK, PART), f32),
            pltpu.VMEM((ROWS, 2, TOK, PART), bf16),
            pltpu.VMEM((ROWS, 2, TOK, PART), bf16),
            pltpu.VMEM((ROWS, TOK, PART), bf16),
            pltpu.VMEM((ROWS, TOK, PART), bf16),
            pltpu.VMEM((ROWS, TOK, PART), bf16),
            pltpu.VMEM((COLS, TOK, PART), bf16),
            pltpu.VMEM((COLS, TOK, PART), bf16),
            pltpu.VMEM((COLS, TOK, PART), bf16),
            pltpu.SemaphoreType.DMA((3,)),
            pair,
            pair,
            eight,
            eight,
            four,
            four,
            eight,
            eight,
            eight,
            eight,
            four,
            four,
        ]
        + [eight] * 17,
        compiler_params=pltpu.CompilerParams(
            collective_id=0, has_side_effects=True, vmem_limit_bytes=44 << 20
        ),
    )(
        queries,
        key_vectors,
        values,
        sink_logit,
        lengths,
        stream,
        out_weight,
        norm_gain.reshape(PART // HDIM, HDIM),
        shared,
        shared_switch.reshape(WIDTH // HDIM, HDIM),
        expert_gate[0].T,
        expert_up[0].T,
        expert_down[0],
        routes.T,
        route_weights.T,
    )


def gathered_body(
    queries,
    key_vectors,
    values,
    sink_logit,
    lengths,
    stream,
    out_weight,
    norm_gain,
    shared_gate,
    shared_up,
    shared_down,
    shared_switch,
    expert_gate,
    expert_up,
    expert_down,
    routes,
    route_weights,
):
    local_tokens = queries.shape[0]
    feature_width = queries.shape[1]
    head_count = feature_width // HDIM
    my_row = lax.axis_index("row")
    positions = my_row * local_tokens + jnp.arange(local_tokens, dtype=jnp.int32)
    lower_bound = lower_bounds(lengths, positions)
    query_heads = queries.reshape(local_tokens, head_count, HDIM)
    score_scale = 1.0 / math.sqrt(HDIM)
    key_value = jnp.stack([key_vectors, values], 0)
    key_piece = lax.all_gather(key_value, "row", axis=1, tiled=True)
    row_max = jnp.broadcast_to(sink_logit[None, :], (local_tokens, head_count))
    denominator = jnp.ones((local_tokens, head_count), jnp.float32)
    numerator = jnp.zeros((local_tokens, head_count, HDIM), jnp.float32)
    needed = key_piece.shape[1]
    key_heads = key_piece[0].reshape(needed, head_count, HDIM)
    value_heads = key_piece[1].reshape(needed, head_count, HDIM)
    scores = (
        jnp.einsum("qhd,khd->qhk", query_heads, key_heads, preferred_element_type=jnp.float32)
        * score_scale
    )
    key_places = jnp.arange(needed, dtype=jnp.int32)
    visible = (
        (key_places[None, :] >= lower_bound[:, None]) & (key_places[None, :] <= positions[:, None])
    )[:, None, :]
    masked = jnp.where(visible, scores, masked_score)
    new_max = jnp.maximum(row_max, jnp.max(masked, axis=2))
    weight = jnp.where(visible, jnp.exp(masked - new_max[:, :, None]), 0.0)
    rescale = jnp.exp(row_max - new_max)
    denominator = denominator * rescale + jnp.sum(weight, axis=2)
    numerator = numerator * rescale[:, :, None] + jnp.einsum(
        "qhk,khd->qhd", weight.astype(jnp.bfloat16), value_heads, preferred_element_type=jnp.float32
    )
    final_max, denominator, numerator = (new_max, denominator, numerator)
    attended = (
        (numerator / denominator[:, :, None])
        .reshape(local_tokens, feature_width)
        .astype(jnp.bfloat16)
    )
    head_terms = jnp.dot(
        attended,
        lax.all_gather(out_weight, "row", axis=1, tiled=True),
        preferred_element_type=jnp.float32,
    )
    mixed_heads = lax.psum_scatter(
        head_terms.astype(jnp.bfloat16), "col", scatter_dimension=1, tiled=True
    ).astype(jnp.float32)
    hidden = (stream.astype(jnp.float32) + mixed_heads).astype(jnp.bfloat16)
    widened = hidden.astype(jnp.float32)
    full_width = lax.axis_size("col") * hidden.shape[1]
    squares = lax.psum(jnp.sum(widened * widened, axis=1), "col")
    row_scale = lax.rsqrt(squares / full_width + norm_eps)
    normed_part = (widened * row_scale[:, None] * norm_gain.astype(jnp.float32)).astype(
        jnp.bfloat16
    )
    normed = lax.all_gather(normed_part, "col", axis=1, tiled=True)
    gate_part = jnp.dot(
        normed,
        lax.all_gather(shared_gate, "row", axis=0, tiled=True),
        preferred_element_type=jnp.float32,
    )
    up_part = jnp.dot(
        normed,
        lax.all_gather(shared_up, "row", axis=0, tiled=True),
        preferred_element_type=jnp.float32,
    )
    shared_act = (jax.nn.silu(gate_part) * up_part).astype(jnp.bfloat16)
    shared_part = jnp.dot(
        shared_act,
        lax.all_gather(shared_down, "row", axis=1, tiled=True),
        preferred_element_type=jnp.float32,
    )
    switch = jax.nn.sigmoid(jnp.dot(normed, shared_switch, preferred_element_type=jnp.float32))
    row_count = lax.axis_size("row")
    fanout = routes.shape[1]
    model_width = normed.shape[1]
    capacity = max(2, min(local_tokens, 3 * local_tokens * fanout // (2 * row_count)))
    flat_routes = routes.reshape(-1)
    onehot = (flat_routes[:, None] == jnp.arange(row_count, dtype=jnp.int32)[None, :]).astype(
        jnp.int32
    )
    before = jnp.cumsum(onehot, axis=0) - onehot
    slot_index = jnp.sum(before * onehot, axis=1)
    target = flat_routes * capacity + slot_index
    owner_row = jnp.arange(local_tokens * fanout, dtype=jnp.int32) // fanout
    source = jnp.full((row_count * capacity,), local_tokens, jnp.int32).at[target].set(owner_row)
    padded = jnp.concatenate([normed, jnp.zeros((1, model_width), jnp.bfloat16)], 0)
    outgoing = padded[source].reshape(row_count, capacity, model_width)
    received = lax.all_to_all(outgoing, "row", split_axis=0, concat_axis=0, tiled=True)
    senders, slot_count, received_width = received.shape
    dispatched = received.reshape(senders * slot_count, received_width)
    gate_out = jnp.dot(dispatched, expert_gate[0], preferred_element_type=jnp.float32)
    up_out = jnp.dot(dispatched, expert_up[0], preferred_element_type=jnp.float32)
    activation = (jax.nn.silu(gate_out) * up_out).astype(jnp.bfloat16)
    partial_out = jnp.dot(activation, expert_down[0], preferred_element_type=jnp.float32).astype(
        jnp.bfloat16
    )
    returned = lax.all_to_all(
        partial_out.reshape(senders, slot_count, received_width),
        "row",
        split_axis=0,
        concat_axis=0,
        tiled=True,
    )
    route_rows = returned.reshape(row_count * capacity, model_width)[target].reshape(
        local_tokens, fanout, model_width
    )
    routed = jnp.zeros((local_tokens, model_width), jnp.float32)
    for route_slot in range(fanout):
        routed = routed + route_weights[:, route_slot][:, None] * route_rows[
            :, route_slot, :
        ].astype(jnp.float32)
    layer_terms = switch[:, None] * shared_part + routed
    summed = lax.psum_scatter(
        layer_terms.astype(jnp.bfloat16), "col", scatter_dimension=1, tiled=True
    ).astype(jnp.float32)
    layer_out = (hidden.astype(jnp.float32) + summed).astype(jnp.bfloat16)
    return (attended, layer_out)


def solution(mesh):
    small = mesh.shape["row"] == ROWS and mesh.shape["col"] == COLS
    return jax.shard_map(
        fused_body if small else gathered_body,
        mesh=mesh,
        in_specs=(
            P("row", "col"),
            P("row", "col"),
            P("row", "col"),
            P("col"),
            P(),
            P("row", "col"),
            P("col", "row"),
            P("col"),
            P("row", "col"),
            P("row", "col"),
            P("col", "row"),
            P(),
            P("row", None, "col"),
            P("row", None, "col"),
            P("row", "col", None),
            P("row", None),
            P("row", None),
        ),
        out_specs=(P("row", "col"), P("row", "col")),
        check_vma=False,
    )
```
